32 devices in a mesh: dp: 4 (over y, core), blk: 4 (over z), ulysses: 2 (over x).
Axes of the slice: x: 2, y: 2, z: 4, core: 2. Of those that a mesh axis runs over, the one named last changes fastest.
Arguments:
- queries: bfloat16 [24576, 2048], P(('dp', 'blk', 'ulysses')), parts along dimension 0, may hold values from -128 to 128
- keys: bfloat16 [24576, 2048], P(('dp', 'blk', 'ulysses')), parts along dimension 0, may hold values from -6 to 6
- values: bfloat16 [24576, 2048], P(('dp', 'blk', 'ulysses')), parts along dimension 0, may hold values from -6 to 6
- rel_bias: float32 [16, 27], replicated, may hold values from -4 to 4
- tile_lists: int32 [16, 8], replicated, may hold values from 0 to 16, as said below
- tile_pos: int32 [16], replicated, may hold values from 0 to 3, as said below
Outputs:
- attended: bfloat16 [24576, 2048], P(('dp', 'blk', 'ulysses')), parts along dimension 0
The draws below stay inside these ranges and needn't reach their ends.
There are 4 independent parts, one for each index of `dp`. The reference program is written for one: setup_inputs(seed, part) draws one part's arguments, and reference() takes and returns one part's arrays. A program takes and returns all parts, laid end to end along the dimension named above; an argument that names none is the same for every part. Nothing has to cross between parts.
Inputs may be any that keep to these rules, and one draw needn't show every extreme that they name: `tile_lists`: row t names the key tiles of query tile t, each once: t itself first, then tiles of t's frame or of the frames just before and after it (frame = tile // 4); named tiles come first and 16 fills the rest of the row. `tile_pos`: the cell (row * 2 + column) of each tile within its frame; the tiles of one frame take each cell once.
All inputs are finite; a program needn't handle non-finite values.
Results may differ from the reference program's by a relative error of at most 0.0035.
Values may be sent and summed in bfloat16 or wider, within the bound.
A program may use at most 128 MiB of HBM per device.

```python
import math
import jax
import jax.numpy as jnp
from jax import lax

H = 16
DH = 128
TILE = 384
GH = 2
GW = 2
NBR = 8
QW = 2048
NFRAMES = 4
NT = 16
SEQ = 6144


def query_key_pair(key):
    base_keys = jnp.clip(jax.random.normal(jax.random.fold_in(key, 101), (SEQ, QW), jnp.float32), -6.0, 6.0)
    base_queries = jnp.clip(3.0 * jax.random.normal(jax.random.fold_in(key, 202), (SEQ, QW), jnp.float32), -18.0, 18.0)
    return (base_queries, base_keys)


def draw_queries(key, part):
    return query_key_pair(key)[0].astype(jnp.bfloat16)


def draw_keys(key, part):
    return query_key_pair(key)[1].astype(jnp.bfloat16)


def draw_tile_lists(key, part):
    frame_tiles = GH * GW
    tile_ids = jnp.arange(NT, dtype=jnp.int32)
    frame_of = tile_ids // frame_tiles
    candidate = jnp.arange(3 * frame_tiles, dtype=jnp.int32)
    cand_frame = frame_of[:, None] - 1 + candidate[None, :] // frame_tiles
    cand_tile = cand_frame * frame_tiles + candidate[None, :] % frame_tiles
    inside = (cand_frame >= 0) & (cand_frame < NFRAMES)
    random_part = jax.random.randint(jax.random.fold_in(key, 1), (NT, 3 * frame_tiles), 0, 65536)
    ranking = random_part * (3 * frame_tiles) + candidate[None, :]
    ranking = jnp.where(cand_tile == tile_ids[:, None], 2 ** 30, ranking)
    ranking = jnp.where(inside, ranking, -1)
    order = jnp.argsort(-ranking, axis=1)
    sorted_tiles = jnp.take_along_axis(cand_tile, order, axis=1)
    heavy = jax.random.randint(jax.random.fold_in(key, 2), (NFRAMES,), 0, 4) == 0
    heavy = heavy | (jnp.arange(NFRAMES) == 1)
    light = jax.random.randint(jax.random.fold_in(key, 3), (NT,), 3, 6)
    wanted = jnp.where(heavy[frame_of], NBR, light)
    available = jnp.sum(inside.astype(jnp.int32), axis=1)
    wanted = jnp.minimum(wanted, available)
    slot_ids = jnp.arange(NBR)
    return jnp.where(slot_ids[None, :] < wanted[:, None], sorted_tiles[:, :NBR], NT).astype(jnp.int32)


def draw_tile_pos(key, part):
    frame_tiles = GH * GW
    ranking = jax.random.randint(jax.random.fold_in(key, 7), (NFRAMES, frame_tiles), 0, 65536) * frame_tiles
    ranking = ranking + jnp.arange(frame_tiles)[None, :]
    return jnp.argsort(ranking, axis=1).astype(jnp.int32).reshape(NT)


def shard_levels(stream_key, extent, cuts, smallest, top_value):
    level = 1.0
    for dim, blocks in cuts:
        heights = jax.random.uniform(jax.random.fold_in(jax.random.fold_in(stream_key, 6), dim), (blocks,), jnp.float32, smallest / len(cuts), top_value / len(cuts))
        level = level * jnp.repeat(jnp.exp(heights), extent[dim] // blocks).reshape((-1,) + (1,) * (len(extent) - 1 - dim))
    return level


def normal_values(rng, dims, spread, bound, cuts=(), kind=jnp.bfloat16):
    entries = jax.random.normal(rng, dims, jnp.float32) * spread
    if len(cuts) > 0:
        entries = shard_levels(rng, dims, cuts, -0.22, 0.18) * entries
    return jnp.clip(entries, min=-bound, max=bound).astype(kind)


def setup_inputs(seed: int = 0, part: int = 0) -> dict:
    splits = jax.random.split(jax.random.key(seed), 7)
    own_keys = jax.random.split(jax.random.fold_in(splits[6], part), 7)
    queries = draw_queries(jax.random.fold_in(jax.random.fold_in(splits[6], part), 71), part)
    keys = draw_keys(jax.random.fold_in(jax.random.fold_in(splits[6], part), 71), part)
    values = normal_values(own_keys[2], (SEQ, QW), 1.0, 6.0, ((0, 8),))
    rel_bias = normal_values(splits[3], (H, 27), 1.0, 4.0, (), jnp.float32)
    tile_lists = draw_tile_lists(jax.random.fold_in(splits[6], 71), part)
    tile_pos = draw_tile_pos(jax.random.fold_in(splits[6], 71), part)
    return dict(queries=queries, keys=keys, values=values, rel_bias=rel_bias, tile_lists=tile_lists, tile_pos=tile_pos)


def reference(queries, keys, values, rel_bias, tile_lists, tile_pos):
    frame_tiles = GH * GW
    query_tiles = queries.reshape(NT, TILE, H, DH)
    key_tiles = keys.reshape(NT, TILE, H, DH)
    value_tiles = values.reshape(NT, TILE, H, DH)
    frame_of = jnp.arange(NT, dtype=jnp.int32) // frame_tiles
    inv_root = 1.0 / math.sqrt(DH)

    def one_tile(tile_index):
        listed = tile_lists[tile_index]
        valid = listed < NT
        safe_ids = jnp.where(valid, listed, 0).astype(jnp.int32)
        key_block = key_tiles[safe_ids].astype(jnp.float32)
        value_block = value_tiles[safe_ids].astype(jnp.float32)
        query_tile = query_tiles[tile_index].astype(jnp.float32)
        scores = jnp.einsum('ihd,njhd->ihnj', query_tile, key_block) * inv_root
        query_cell = tile_pos[tile_index]
        key_cell = tile_pos[safe_ids]
        offset = (frame_of[safe_ids] - frame_of[tile_index] + 1) * 9
        offset = offset + (key_cell // GW - query_cell // GW + 1) * 3
        offset = offset + (key_cell % GW - query_cell % GW + 1)
        offset = jnp.clip(offset, 0, 26).astype(jnp.int32)
        head_bias = rel_bias[:, offset]
        scores = scores + head_bias[None, :, :, None]
        keep_mask = valid[None, None, :, None]
        scores = jnp.where(keep_mask, scores, -1e+30)
        row_max = lax.optimization_barrier(jnp.max(scores, axis=(2, 3), keepdims=True))
        weights = jnp.where(keep_mask, jnp.exp(scores - row_max), 0.0)
        row_total = lax.optimization_barrier(jnp.sum(weights, axis=(2, 3)))
        rounded = lax.optimization_barrier(weights.astype(jnp.bfloat16)).astype(jnp.float32)
        mixed = jnp.einsum('ihnj,njhd->ihd', rounded, value_block) / row_total[..., None]
        return mixed.astype(jnp.bfloat16)
    attended = lax.map(one_tile, jnp.arange(NT, dtype=jnp.int32))
    return attended.reshape(SEQ, QW)
```

```python
import functools
import math

import jax
import jax.numpy as jnp
from jax import lax
from jax.experimental import pallas as pl
from jax.experimental.pallas import tpu as pltpu
from jax.sharding import PartitionSpec as P

H = 16
DH = 128
TILE = 384
GH = 2
GW = 2
LOG2E = 1.4426950408889634
MESH = pl.DeviceIdType.MESH


def attention_kernel(n, blk_count, groups, tokens, slots, *refs):
    named_ref, pos_ref, table_ref, q_ref, k_ref, v_ref, out_ref = refs[:7]
    refs = refs[7:]
    k_bufs = refs[:groups]
    v_bufs = refs[groups : 2 * groups]
    q_bufs = refs[2 * groups : 3 * groups]
    o_bufs = refs[3 * groups : 4 * groups]
    lists_ref, bias_ref, s_buf, w_buf, local_sems, x_send, x_recv, z_send, z_recv, o_send, o_recv = refs[4 * groups :]
    frame = tokens * n
    head_cols = groups * DH
    rank = lax.axis_index("ulysses")
    blk = lax.axis_index("blk")
    has_up = blk < blk_count - 1
    has_down = blk > 0
    scale = LOG2E / math.sqrt(DH)
    inputs = (k_ref, v_ref, q_ref)

    unit = math.gcd(tokens, TILE)
    parts = TILE // unit
    held = tokens // unit
    frame_tiles = frame // TILE
    total_tiles = pos_ref.shape[0]

    def rows(frame_index, owner):
        return pl.ds(frame_index * (frame // unit) + owner * held, held)

    def flat(owner):
        return pl.ds(pl.multiple_of(owner * tokens, 64), tokens)

    def lanes(owner, g):
        return pl.ds(pl.multiple_of(owner * head_cols + g * DH, DH), DH)

    def cut(which, owner, g):
        if which == 2:
            return q_ref.at[:, lanes(owner, g)]
        return inputs[which].at[:, :, lanes(owner, g)]

    def home(which, g, owner):
        if which == 2:
            return q_bufs[g].at[flat(owner)]
        return (k_bufs, v_bufs)[which][g].at[rows(1, owner)]

    def local(which, g):
        return pltpu.make_async_copy(
            cut(which, rank, g), home(which, g, rank), local_sems.at[which, g]
        )

    def across(which, g, d):
        target = lax.rem(rank + d, n)
        return pltpu.make_async_remote_copy(
            src_ref=cut(which, target, g),
            dst_ref=home(which, g, rank),
            send_sem=x_send.at[which, g, d],
            recv_sem=x_recv.at[which, g, d],
            device_id={"ulysses": target},
            device_id_type=MESH,
        )

    def halo(which, g, d, way):
        owner = lax.rem(rank + (n - d), n)
        source = home(which, g, owner) if d else cut(which, rank, g)
        return pltpu.make_async_remote_copy(
            src_ref=source,
            dst_ref=(k_bufs, v_bufs)[which][g].at[rows(2 * way, owner)],
            send_sem=z_send.at[way, which, g, d],
            recv_sem=z_recv.at[way, which, g, d],
            device_id={"blk": blk - 1 if way else blk + 1},
            device_id_type=MESH,
        )

    def give(g, u):
        owner, at = lax.div(u, held), lax.rem(u, held)
        return pltpu.make_async_remote_copy(
            src_ref=o_bufs[g].at[u],
            dst_ref=out_ref.at[rank * groups + g, at],
            send_sem=o_send.at[g, u],
            recv_sem=o_recv.at[g, rank, at],
            device_id={"ulysses": owner},
            device_id_type=MESH,
        )

    def taken(g, owner, at):
        return pltpu.make_async_remote_copy(
            src_ref=o_bufs[g].at[at],
            dst_ref=out_ref.at[owner * groups + g, at],
            send_sem=o_send.at[g, at],
            recv_sem=o_recv.at[g, owner, at],
            device_id={"ulysses": owner},
            device_id_type=MESH,
        )

    def start_halo(which, g, ds):
        for way, present in ((0, has_up), (1, has_down)):
            @pl.when(present)
            def _():
                for d in ds:
                    halo(which, g, d, way).start()

    def relay(which, g):
        for d in range(1, n):
            across(which, g, d).wait_recv()
        start_halo(which, g, range(1, n))

    def arrive(which, g):
        for way, present in ((0, has_down), (1, has_up)):
            @pl.when(present)
            def _():
                for d in range(n):
                    halo(which, g, d, way).wait_recv()

    barrier = pltpu.get_barrier_semaphore()
    for d in range(1, n):
        pl.semaphore_signal(
            barrier, inc=1, device_id={"ulysses": lax.rem(rank + d, n)}, device_id_type=MESH
        )
    @pl.when(has_up)
    def _():
        pl.semaphore_signal(barrier, inc=1, device_id={"blk": blk + 1}, device_id_type=MESH)
    @pl.when(has_down)
    def _():
        pl.semaphore_signal(barrier, inc=1, device_id={"blk": blk - 1}, device_id_type=MESH)
    below = (blk + blk_count - 1) // blk_count
    above = (2 * blk_count - 2 - blk) // blk_count
    pl.semaphore_wait(barrier, n - 1 + below + above)

    steps = [(0, 0)]
    for g in range(groups):
        if g + 1 < groups:
            steps.append((0, g + 1))
        steps.append((1, g))

    for at, (which, g) in enumerate(steps):
        for w in (which, 2) if which == 0 else (which,):
            for d in range(1, n):
                across(w, g, d).start()
        if at < 2:
            start_halo(which, g, range(1))
    for which, g in steps:
        local(which, g).start()
        if which == 0:
            local(2, g).start()

    def tabulate(at, _):
        t, i = lax.div(at, slots), lax.rem(at, slots)
        tile = blk * frame_tiles + t
        valid = named_ref[i, tile] < total_tiles
        safe = jnp.where(valid, named_ref[i, tile], tile)
        lists_ref[t, i] = jnp.clip(safe - (blk - 1) * frame_tiles, 0, 3 * frame_tiles - 1)
        key_cell, query_cell = pos_ref[safe], pos_ref[tile]
        offset = (lax.div(safe, frame_tiles) - blk + 1) * 9
        offset = offset + (lax.div(key_cell, GW) - lax.div(query_cell, GW) + 1) * 3
        offset = offset + (lax.rem(key_cell, GW) - lax.rem(query_cell, GW) + 1)
        offset = jnp.clip(offset, 0, 26)
        for g in range(groups):
            value = table_ref[rank * groups + g, offset] * LOG2E
            bias_ref[t, i, g] = jnp.where(valid, value, -1e30)
        return 0

    lax.fori_loop(0, frame_tiles * slots, tabulate, 0)

    pairs = slots // 2
    ones = jnp.ones((2 * TILE, DH), jnp.bfloat16)
    first = lax.div(lax.rem(rank + 1, n) * tokens, TILE)

    def listed(buf, t, p):
        return jnp.concatenate(
            [
                buf[lists_ref[t, 2 * p + i] * parts + j]
                for i in range(2)
                for j in range(parts)
            ],
            axis=0,
        )

    def weigh(g):
        def tile_body(t, _):
            here = pl.ds(pl.multiple_of(t * TILE, TILE), TILE)

            def score_pair(p, top):
                s = lax.dot_general(
                    q_bufs[g][here, :],
                    listed(k_bufs[g], t, p),
                    (((1,), (1,)), ((), ())),
                    preferred_element_type=jnp.float32,
                )
                s_buf[p] = s
                for i in range(2):
                    m = s[:, i * TILE : i * TILE + DH]
                    for c in range(1, TILE // DH):
                        m = jnp.maximum(m, s[:, i * TILE + c * DH : i * TILE + (c + 1) * DH])
                    top = jnp.maximum(top, m * scale + bias_ref[t, 2 * p + i, g])
                return top

            top = lax.fori_loop(0, pairs, score_pair, jnp.full((TILE, DH), -3e38, jnp.float32))
            top = jnp.broadcast_to(jnp.max(top, axis=1, keepdims=True), (TILE, DH))

            def weigh_pair(p, top):
                for i in range(2):
                    shift = bias_ref[t, 2 * p + i, g] - top
                    for c in range(TILE // DH):
                        span = slice(i * TILE + c * DH, i * TILE + (c + 1) * DH)
                        w = jnp.exp2(s_buf[p, :, span] * scale + shift)
                        w_buf[g % 2, t * pairs + p, :, span] = w.astype(jnp.bfloat16)
                return top

            lax.fori_loop(0, pairs, weigh_pair, top)
            return 0

        lax.fori_loop(0, frame_tiles, tile_body, 0)

    def mix(g):
        def tile_body(step, _):
            t = lax.rem(step + first, frame_tiles)
            total = None
            for p in range(pairs):
                value = jnp.concatenate([listed(v_bufs[g], t, p), ones], axis=1)
                part = jnp.dot(
                    w_buf[g % 2, t * pairs + p], value, preferred_element_type=jnp.float32
                )
                total = part if total is None else total + part
            result = (total[:, :DH] / total[:, DH:]).astype(jnp.bfloat16)
            for j in range(parts):
                u = t * parts + j
                piece = result[j * unit : (j + 1) * unit]
                owner = lax.div(u, held)

                @pl.when(owner == rank)
                def _():
                    out_ref[rank * groups + g, lax.rem(u, held)] = piece

                @pl.when(owner != rank)
                def _():
                    o_bufs[g][u] = piece
                    give(g, u).start()
            return 0

        lax.fori_loop(0, frame_tiles, tile_body, 0)

    relay(*steps[0])
    for at, (which, g) in enumerate(steps):
        if at + 1 < len(steps):
            relay(*steps[at + 1])
        if at + 2 < len(steps):
            start_halo(*steps[at + 2], range(1))
        local(which, g).wait()
        if which == 0:
            local(2, g).wait()
            for d in range(1, n):
                across(2, g, d).wait_recv()
        arrive(which, g)
        if which == 0:
            weigh(g)
        else:
            mix(g)

    for g in range(groups):
        for d in range(1, n):
            for which in range(3):
                across(which, g, d).wait_send()
            for at in range(held):
                taken(g, lax.rem(rank + d, n), at).wait_recv()
        for u in range(n * held):
            @pl.when(rank != u // held)
            def _():
                give(g, u).wait_send()
        for way, present in ((0, has_up), (1, has_down)):
            @pl.when(present)
            def _():
                for d in range(n):
                    for which in range(2):
                        halo(which, g, d, way).wait_send()


def write_kernel(x_ref, out_ref, sems):
    heads, held, unit, width = x_ref.shape

    def copy(h, at):
        return pltpu.make_async_copy(
            x_ref.at[h, at],
            out_ref.at[at, :, pl.ds(h * width, width)],
            sems.at[h, at],
        )

    for h in range(heads):
        for at in range(held):
            copy(h, at).start()
    for h in range(heads):
        for at in range(held):
            copy(h, at).wait()


def on_device(queries, keys, values, rel_bias, tile_lists, tile_pos):
    n = lax.axis_size("ulysses")
    blk_count = lax.axis_size("blk")
    groups = H // n
    tokens = queries.shape[0]
    frame_tokens = tokens * n
    frame_tiles = frame_tokens // TILE
    slots = tile_lists.shape[1]

    smem = pl.BlockSpec(memory_space=pltpu.SMEM)
    hbm = pl.BlockSpec(memory_space=pl.ANY)
    vmem = lambda *shape: [pltpu.VMEM((*shape, DH), jnp.bfloat16)] * groups
    unit = math.gcd(tokens, TILE)
    held = tokens // unit
    split = (held, unit, queries.shape[1])
    dma = pltpu.SemaphoreType.DMA
    by_head = pl.pallas_call(
        functools.partial(attention_kernel, n, blk_count, groups, tokens, slots),
        out_shape=pltpu.VMEM((H, held, unit, DH), jnp.bfloat16),
        in_specs=[smem, smem, smem, hbm, hbm, hbm],
        out_specs=pl.BlockSpec(memory_space=pltpu.VMEM),
        scratch_shapes=[
            *vmem(3 * frame_tokens // unit, unit),
            *vmem(3 * frame_tokens // unit, unit),
            *vmem(frame_tokens),
            *vmem(frame_tokens // unit, unit),
            pltpu.SMEM((frame_tiles, slots), jnp.int32),
            pltpu.SMEM((frame_tiles, slots, groups), jnp.float32),
            pltpu.VMEM((slots // 2, TILE, 2 * TILE), jnp.float32),
            pltpu.VMEM((2, frame_tiles * slots // 2, TILE, 2 * TILE), jnp.bfloat16),
            dma((3, groups)),
            dma((3, groups, n)),
            dma((3, groups, n)),
            dma((2, 2, groups, n)),
            dma((2, 2, groups, n)),
            dma((groups, n * held)),
            dma((groups, n, held)),
        ],
        compiler_params=pltpu.CompilerParams(
            collective_id=0, has_side_effects=True, vmem_limit_bytes=54 * 1024 * 1024
        ),
        name="attend",
    )(tile_lists.T, tile_pos, rel_bias, queries, keys.reshape(split), values.reshape(split))
    out = pl.pallas_call(
        write_kernel,
        out_shape=jax.ShapeDtypeStruct(split, jnp.bfloat16),
        in_specs=[hbm],
        out_specs=hbm,
        scratch_shapes=[dma((H, held))],
        compiler_params=pltpu.CompilerParams(vmem_limit_bytes=1024 * 1024),
        name="write",
    )(by_head)
    return out.reshape(queries.shape)


def solution(mesh):
    return jax.shard_map(
        on_device,
        mesh=mesh,
        in_specs=(
            P(("dp", "blk", "ulysses"), None),
            P(("dp", "blk", "ulysses"), None),
            P(("dp", "blk", "ulysses"), None),
            P(),
            P(),
            P(),
        ),
        out_specs=P(("dp", "blk", "ulysses"), None),
        check_vma=False,
    )
```

```python
import functools
import math

import jax
import jax.numpy as jnp
from jax import lax
from jax.experimental import pallas as pl
from jax.experimental.pallas import tpu as pltpu
from jax.sharding import PartitionSpec as P

H = 16
DH = 128
TILE = 384
GH = 2
GW = 2
LOG2E = 1.4426950408889634
MESH = pl.DeviceIdType.MESH


def attention_kernel(n, blk_count, groups, tokens, slots, *refs):
    named_hbm, pos_hbm, table_hbm, q_ref, k_ref, v_ref, out_ref = refs[:7]
    refs = refs[7:]
    k_bufs = refs[:groups]
    v_bufs = refs[groups : 2 * groups]
    q_bufs = refs[2 * groups : 3 * groups]
    o_bufs = refs[3 * groups : 4 * groups]
    named_ref, pos_ref, table_ref, small_sems, lists_ref, bias_ref, s_buf, w_buf, local_sems, x_send, x_recv, z_send, z_recv, o_send, o_recv = refs[4 * groups :]
    frame = tokens * n
    head_cols = groups * DH
    rank = lax.axis_index("ulysses")
    blk = lax.axis_index("blk")
    has_up = blk < blk_count - 1
    has_down = blk > 0
    scale = LOG2E / math.sqrt(DH)
    inputs = (k_ref, v_ref, q_ref)

    unit = math.gcd(tokens, TILE)
    parts = TILE // unit
    held = tokens // unit
    frame_tiles = frame // TILE
    total_tiles = pos_ref.shape[0]

    def rows(frame_index, owner):
        return pl.ds(frame_index * (frame // unit) + owner * held, held)

    def flat(owner):
        return pl.ds(pl.multiple_of(owner * tokens, 64), tokens)

    def lanes(owner, g):
        return pl.ds(pl.multiple_of(owner * head_cols + g * DH, DH), DH)

    def cut(which, owner, g):
        if which == 2:
            return q_ref.at[:, lanes(owner, g)]
        return inputs[which].at[:, :, lanes(owner, g)]

    def home(which, g, owner):
        if which == 2:
            return q_bufs[g].at[flat(owner)]
        return (k_bufs, v_bufs)[which][g].at[rows(1, owner)]

    def local(which, g):
        return pltpu.make_async_copy(
            cut(which, rank, g), home(which, g, rank), local_sems.at[which, g]
        )

    def across(which, g, d):
        target = lax.rem(rank + d, n)
        return pltpu.make_async_remote_copy(
            src_ref=cut(which, target, g),
            dst_ref=home(which, g, rank),
            send_sem=x_send.at[which, g, d],
            recv_sem=x_recv.at[which, g, d],
            device_id={"ulysses": target},
            device_id_type=MESH,
        )

    def halo(which, g, d, way):
        owner = lax.rem(rank + (n - d), n)
        source = home(which, g, owner) if d else cut(which, rank, g)
        return pltpu.make_async_remote_copy(
            src_ref=source,
            dst_ref=(k_bufs, v_bufs)[which][g].at[rows(2 * way, owner)],
            send_sem=z_send.at[way, which, g, d],
            recv_sem=z_recv.at[way, which, g, d],
            device_id={"blk": blk - 1 if way else blk + 1},
            device_id_type=MESH,
        )

    def give(g, u):
        owner, at = lax.div(u, held), lax.rem(u, held)
        return pltpu.make_async_remote_copy(
            src_ref=o_bufs[g].at[u],
            dst_ref=out_ref.at[at, :, lanes(rank, g)],
            send_sem=o_send.at[g, u],
            recv_sem=o_recv.at[g, rank, at],
            device_id={"ulysses": owner},
            device_id_type=MESH,
        )

    def taken(g, owner, at):
        return pltpu.make_async_remote_copy(
            src_ref=o_bufs[g].at[at],
            dst_ref=out_ref.at[at, :, lanes(owner, g)],
            send_sem=o_send.at[g, at],
            recv_sem=o_recv.at[g, owner, at],
            device_id={"ulysses": owner},
            device_id_type=MESH,
        )

    def start_halo(which, g, ds):
        for way, present in ((0, has_up), (1, has_down)):
            @pl.when(present)
            def _():
                for d in ds:
                    halo(which, g, d, way).start()

    def relay(which, g):
        for d in range(1, n):
            across(which, g, d).wait_recv()
        start_halo(which, g, range(1, n))

    def arrive(which, g):
        for way, present in ((0, has_down), (1, has_up)):
            @pl.when(present)
            def _():
                for d in range(n):
                    halo(which, g, d, way).wait_recv()

    small = [
        pltpu.make_async_copy(source, target, small_sems.at[i])
        for i, (source, target) in enumerate(
            ((named_hbm, named_ref), (pos_hbm, pos_ref), (table_hbm, table_ref))
        )
    ]

    barrier = pltpu.get_barrier_semaphore()
    for d in range(1, n):
        pl.semaphore_signal(
            barrier, inc=1, device_id={"ulysses": lax.rem(rank + d, n)}, device_id_type=MESH
        )
    @pl.when(has_up)
    def _():
        pl.semaphore_signal(barrier, inc=1, device_id={"blk": blk + 1}, device_id_type=MESH)
    @pl.when(has_down)
    def _():
        pl.semaphore_signal(barrier, inc=1, device_id={"blk": blk - 1}, device_id_type=MESH)
    below = (blk + blk_count - 1) // blk_count
    above = (2 * blk_count - 2 - blk) // blk_count
    pl.semaphore_wait(barrier, n - 1 + below + above)

    steps = [(0, 0)]
    for g in range(groups):
        if g + 1 < groups:
            steps.append((0, g + 1))
        steps.append((1, g))

    sent = []
    for at, (which, g) in enumerate(steps):
        sent.append((which, g))
        if which == 0 and g > 1:
            sent.append((2, g - 1))
        if (which, g) == (1, 0):
            sent.append((2, 0))
    sent += [(2, g) for g in range(1, groups) if (2, g) not in sent]
    if groups > 1:
        sent[-2:] = sent[:-3:-1]

    ahead = min(4, len(steps))
    leads = lax.rem(lax.axis_index("dp"), 2) == 1

    @pl.when(leads)
    def _():
        for at in range(ahead):
            start_halo(*steps[at], range(1))

    for which, g in sent:
        for d in range(1, n):
            across(which, g, d).start()
    for copy in small:
        copy.start()
    for which, g in sent:
        local(which, g).start()

    for copy in small:
        copy.wait()

    def tabulate(at, _):
        t, i = lax.div(at, slots), lax.rem(at, slots)
        tile = blk * frame_tiles + t
        valid = named_ref[i, tile] < total_tiles
        safe = jnp.where(valid, named_ref[i, tile], tile)
        lists_ref[t, i] = jnp.clip(safe - (blk - 1) * frame_tiles, 0, 3 * frame_tiles - 1)
        key_cell, query_cell = pos_ref[safe], pos_ref[tile]
        offset = (lax.div(safe, frame_tiles) - blk + 1) * 9
        offset = offset + (lax.div(key_cell, GW) - lax.div(query_cell, GW) + 1) * 3
        offset = offset + (lax.rem(key_cell, GW) - lax.rem(query_cell, GW) + 1)
        offset = jnp.clip(offset, 0, 26)
        for g in range(groups):
            value = table_ref[rank * groups + g, offset] * LOG2E
            bias_ref[t, i, g] = jnp.where(valid, value, -1e30)
        return 0

    lax.fori_loop(0, frame_tiles * slots, tabulate, 0)

    @pl.when(jnp.logical_not(leads))
    def _():
        for own in range(ahead):
            start_halo(*steps[own], range(1))

    for at in range(ahead - 1):
        for d in range(1, n):
            across(*steps[at], d).wait_recv()
        start_halo(*steps[at], range(1, n))


    pairs = slots // 2
    ones = jnp.ones((2 * TILE, DH), jnp.bfloat16)
    first = lax.div(lax.rem(rank + 1, n) * tokens, TILE)

    def listed(buf, t, p):
        return jnp.concatenate(
            [
                buf[lists_ref[t, 2 * p + i] * parts + j]
                for i in range(2)
                for j in range(parts)
            ],
            axis=0,
        )

    def weigh(g):
        def tile_body(t, _):
            here = pl.ds(pl.multiple_of(t * TILE, TILE), TILE)
            top = jnp.full((TILE, DH), -3e38, jnp.float32)
            for p in range(pairs):
                s = lax.dot_general(
                    q_bufs[g][here, :],
                    listed(k_bufs[g], t, p),
                    (((1,), (1,)), ((), ())),
                    preferred_element_type=jnp.float32,
                )
                s_buf[p] = s
                for i in range(2):
                    m = s[:, i * TILE : i * TILE + DH]
                    for c in range(1, TILE // DH):
                        m = jnp.maximum(m, s[:, i * TILE + c * DH : i * TILE + (c + 1) * DH])
                    top = jnp.maximum(top, m * scale + bias_ref[t, 2 * p + i, g])
            top = jnp.broadcast_to(jnp.max(top, axis=1, keepdims=True), (TILE, DH))
            for p in range(pairs):
                for i in range(2):
                    shift = bias_ref[t, 2 * p + i, g] - top
                    for c in range(TILE // DH):
                        span = slice(i * TILE + c * DH, i * TILE + (c + 1) * DH)
                        w = jnp.exp2(s_buf[p, :, span] * scale + shift)
                        w_buf[g % 2, t * pairs + p, :, span] = w.astype(jnp.bfloat16)
            return 0

        lax.fori_loop(0, frame_tiles, tile_body, 0)

    def mix(g):
        def tile_body(step, _):
            t = lax.rem(step + first, frame_tiles)
            total = None
            for p in range(pairs):
                value = jnp.concatenate([listed(v_bufs[g], t, p), ones], axis=1)
                part = jnp.dot(
                    w_buf[g % 2, t * pairs + p], value, preferred_element_type=jnp.float32
                )
                total = part if total is None else total + part
            result = (total[:, :DH] / total[:, DH:]).astype(jnp.bfloat16)
            for j in range(parts):
                u = t * parts + j
                piece = result[j * unit : (j + 1) * unit]
                owner = lax.div(u, held)

                @pl.when(owner == rank)
                def _():
                    out_ref[lax.rem(u, held), :, lanes(rank, g)] = piece

                @pl.when(owner != rank)
                def _():
                    o_bufs[g][u] = piece
                    give(g, u).start()
            return 0

        lax.fori_loop(0, frame_tiles, tile_body, 0)

    def drain_return(heads):
        for g in heads:
            for d in range(1, n):
                for at in range(held):
                    taken(g, lax.rem(rank + d, n), at).wait_recv()
            for u in range(n * held):
                @pl.when(rank != u // held)
                def _():
                    give(g, u).wait_send()

    def drain_halo(done):
        for way, present in ((0, has_up), (1, has_down)):
            @pl.when(present)
            def _():
                for which, g in done:
                    for d in range(n):
                        halo(which, g, d, way).wait_send()

    for at, (which, g) in enumerate(steps):
        if at + ahead - 1 < len(steps):
            relay(*steps[at + ahead - 1])
        if at + ahead < len(steps):
            start_halo(*steps[at + ahead], range(1))
        local(which, g).wait()
        if which == 0:
            local(2, g).wait()
            for d in range(1, n):
                across(2, g, d).wait_recv()
        if at == len(steps) - 1:
            for done in range(groups):
                for d in range(1, n):
                    for part in range(3):
                        across(part, done, d).wait_send()
            drain_return(range(max(groups - 2, 0)))
            drain_halo(steps[:-ahead])
        arrive(which, g)
        if which == 0:
            weigh(g)
        else:
            mix(g)

    drain_return(range(max(groups - 2, 0), groups))
    drain_halo(steps[-ahead:])


def write_kernel(x_ref, out_ref, sems):
    count = sems.shape[0]
    width = x_ref.shape[2] // count

    def copy(i):
        part = pl.ds(i * width, width)
        return pltpu.make_async_copy(x_ref.at[:, :, part], out_ref.at[:, :, part], sems.at[i])

    for i in range(count):
        copy(i).start()
    for i in range(count):
        copy(i).wait()


def on_device(queries, keys, values, rel_bias, tile_lists, tile_pos):
    n = lax.axis_size("ulysses")
    blk_count = lax.axis_size("blk")
    groups = H // n
    tokens = queries.shape[0]
    frame_tokens = tokens * n
    frame_tiles = frame_tokens // TILE
    slots = tile_lists.shape[1]

    hbm = pl.BlockSpec(memory_space=pl.ANY)
    vmem = lambda *shape: [pltpu.VMEM((*shape, DH), jnp.bfloat16)] * groups
    unit = math.gcd(tokens, TILE)
    held = tokens // unit
    split = (held, unit, queries.shape[1])
    dma = pltpu.SemaphoreType.DMA
    by_head = pl.pallas_call(
        functools.partial(attention_kernel, n, blk_count, groups, tokens, slots),
        out_shape=pltpu.VMEM(split, jnp.bfloat16),
        in_specs=[hbm] * 6,
        out_specs=pl.BlockSpec(memory_space=pltpu.VMEM),
        scratch_shapes=[
            *vmem(3 * frame_tokens // unit, unit),
            *vmem(3 * frame_tokens // unit, unit),
            *vmem(frame_tokens),
            *vmem(frame_tokens // unit, unit),
            pltpu.SMEM(tile_lists.shape[::-1], jnp.int32),
            pltpu.SMEM(tile_pos.shape, jnp.int32),
            pltpu.SMEM(rel_bias.shape, jnp.float32),
            dma((3,)),
            pltpu.SMEM((frame_tiles, slots), jnp.int32),
            pltpu.SMEM((frame_tiles, slots, groups), jnp.float32),
            pltpu.VMEM((slots // 2, TILE, 2 * TILE), jnp.float32),
            pltpu.VMEM((2, frame_tiles * slots // 2, TILE, 2 * TILE), jnp.bfloat16),
            dma((3, groups)),
            dma((3, groups, n)),
            dma((3, groups, n)),
            dma((2, 2, groups, n)),
            dma((2, 2, groups, n)),
            dma((groups, n * held)),
            dma((groups, n, held)),
        ],
        compiler_params=pltpu.CompilerParams(
            collective_id=0, has_side_effects=True, vmem_limit_bytes=54 * 1024 * 1024
        ),
        name="attend",
    )(tile_lists.T, tile_pos, rel_bias, queries, keys.reshape(split), values.reshape(split))
    out = pl.pallas_call(
        write_kernel,
        out_shape=jax.ShapeDtypeStruct(split, jnp.bfloat16),
        in_specs=[hbm],
        out_specs=hbm,
        scratch_shapes=[dma((4,))],
        compiler_params=pltpu.CompilerParams(vmem_limit_bytes=1024 * 1024),
        name="write",
    )(by_head)
    return out.reshape(queries.shape)


def solution(mesh):
    return jax.shard_map(
        on_device,
        mesh=mesh,
        in_specs=(
            P(("dp", "blk", "ulysses"), None),
            P(("dp", "blk", "ulysses"), None),
            P(("dp", "blk", "ulysses"), None),
            P(),
            P(),
            P(),
        ),
        out_specs=P(("dp", "blk", "ulysses"), None),
        check_vma=False,
    )
```

```python
import functools
import math

import jax
import jax.numpy as jnp
from jax import lax
from jax.experimental import pallas as pl
from jax.experimental.pallas import tpu as pltpu
from jax.sharding import PartitionSpec as P

H = 16
DH = 128
TILE = 384
GH = 2
GW = 2
LOG2E = 1.4426950408889634
MESH = pl.DeviceIdType.MESH


def attention_kernel(n, blk_count, groups, tokens, slots, *refs):
    named_hbm, pos_hbm, table_hbm, q_ref, k_ref, v_ref, out_ref = refs[:7]
    refs = refs[7:]
    k_bufs = refs[:groups]
    v_bufs = refs[groups : 2 * groups]
    q_bufs = refs[2 * groups : 3 * groups]
    o_bufs = refs[3 * groups : 4 * groups]
    named_ref, pos_ref, table_ref, small_sems, lists_ref, bias_ref, s_buf, w_buf, local_sems, x_send, x_recv, z_send, z_recv, o_send, o_recv = refs[4 * groups :]
    frame = tokens * n
    head_cols = groups * DH
    rank = lax.axis_index("ulysses")
    blk = lax.axis_index("blk")
    has_up = blk < blk_count - 1
    has_down = blk > 0
    scale = LOG2E / math.sqrt(DH)
    inputs = (k_ref, v_ref, q_ref)

    unit = math.gcd(tokens, TILE)
    parts = TILE // unit
    held = tokens // unit
    frame_tiles = frame // TILE
    total_tiles = pos_ref.shape[0]

    def rows(frame_index, owner):
        return pl.ds(frame_index * (frame // unit) + owner * held, held)

    def flat(owner):
        return pl.ds(pl.multiple_of(owner * tokens, 64), tokens)

    def lanes(owner, g):
        return pl.ds(pl.multiple_of(owner * head_cols + g * DH, DH), DH)

    def cut(which, owner, g):
        if which == 2:
            return q_ref.at[:, lanes(owner, g)]
        return inputs[which].at[:, :, lanes(owner, g)]

    def home(which, g, owner):
        if which == 2:
            return q_bufs[g].at[flat(owner)]
        return (k_bufs, v_bufs)[which][g].at[rows(1, owner)]

    def local(which, g):
        return pltpu.make_async_copy(
            cut(which, rank, g), home(which, g, rank), local_sems.at[which, g]
        )

    def across(which, g, d):
        target = lax.rem(rank + d, n)
        return pltpu.make_async_remote_copy(
            src_ref=cut(which, target, g),
            dst_ref=home(which, g, rank),
            send_sem=x_send.at[which, g, d],
            recv_sem=x_recv.at[which, g, d],
            device_id={"ulysses": target},
            device_id_type=MESH,
        )

    def halo(which, g, d, way):
        owner = lax.rem(rank + (n - d), n)
        source = home(which, g, owner) if d else cut(which, rank, g)
        return pltpu.make_async_remote_copy(
            src_ref=source,
            dst_ref=(k_bufs, v_bufs)[which][g].at[rows(2 * way, owner)],
            send_sem=z_send.at[way, which, g, d],
            recv_sem=z_recv.at[way, which, g, d],
            device_id={"blk": blk - 1 if way else blk + 1},
            device_id_type=MESH,
        )

    def give(g, u):
        owner, at = lax.div(u, held), lax.rem(u, held)
        return pltpu.make_async_remote_copy(
            src_ref=o_bufs[g].at[u],
            dst_ref=out_ref.at[at, :, lanes(rank, g)],
            send_sem=o_send.at[g, u],
            recv_sem=o_recv.at[g, rank, at],
            device_id={"ulysses": owner},
            device_id_type=MESH,
        )

    def taken(g, owner, at):
        return pltpu.make_async_remote_copy(
            src_ref=o_bufs[g].at[at],
            dst_ref=out_ref.at[at, :, lanes(owner, g)],
            send_sem=o_send.at[g, at],
            recv_sem=o_recv.at[g, owner, at],
            device_id={"ulysses": owner},
            device_id_type=MESH,
        )

    def start_halo(which, g, ds):
        for way, present in ((0, has_up), (1, has_down)):
            @pl.when(present)
            def _():
                for d in ds:
                    halo(which, g, d, way).start()

    def relay(which, g):
        for d in range(1, n):
            across(which, g, d).wait_recv()
        start_halo(which, g, range(1, n))

    def arrive(which, g):
        for way, present in ((0, has_down), (1, has_up)):
            @pl.when(present)
            def _():
                for d in range(n):
                    halo(which, g, d, way).wait_recv()

    small = [
        pltpu.make_async_copy(source, target, small_sems.at[i])
        for i, (source, target) in enumerate(
            ((named_hbm, named_ref), (pos_hbm, pos_ref), (table_hbm, table_ref))
        )
    ]

    barrier = pltpu.get_barrier_semaphore()
    for d in range(1, n):
        pl.semaphore_signal(
            barrier, inc=1, device_id={"ulysses": lax.rem(rank + d, n)}, device_id_type=MESH
        )
    @pl.when(has_up)
    def _():
        pl.semaphore_signal(barrier, inc=1, device_id={"blk": blk + 1}, device_id_type=MESH)
    @pl.when(has_down)
    def _():
        pl.semaphore_signal(barrier, inc=1, device_id={"blk": blk - 1}, device_id_type=MESH)
    below = (blk + blk_count - 1) // blk_count
    above = (2 * blk_count - 2 - blk) // blk_count
    pl.semaphore_wait(barrier, n - 1 + below + above)

    steps = [(0, 0)]
    for g in range(groups):
        if g + 1 < groups:
            steps.append((0, g + 1))
        steps.append((1, g))

    sent = []
    for at, (which, g) in enumerate(steps):
        sent.append((which, g))
        if which == 0 and g > 1:
            sent.append((2, g - 1))
        if (which, g) == (1, 0):
            sent.append((2, 0))
    sent += [(2, g) for g in range(1, groups) if (2, g) not in sent]
    if groups > 1:
        sent[-2:] = sent[:-3:-1]

    ahead = min(6, len(steps))
    leads = lax.rem(lax.axis_index("dp"), 2) == 1

    @pl.when(leads)
    def _():
        for at in range(ahead):
            start_halo(*steps[at], range(1))

    for which, g in sent:
        for d in range(1, n):
            across(which, g, d).start()
    for copy in small:
        copy.start()
    for which, g in sent:
        local(which, g).start()

    for copy in small:
        copy.wait()

    def tabulate(at, _):
        t, i = lax.div(at, slots), lax.rem(at, slots)
        tile = blk * frame_tiles + t
        valid = named_ref[i, tile] < total_tiles
        safe = jnp.where(valid, named_ref[i, tile], tile)
        lists_ref[t, i] = jnp.clip(safe - (blk - 1) * frame_tiles, 0, 3 * frame_tiles - 1)
        key_cell, query_cell = pos_ref[safe], pos_ref[tile]
        offset = (lax.div(safe, frame_tiles) - blk + 1) * 9
        offset = offset + (lax.div(key_cell, GW) - lax.div(query_cell, GW) + 1) * 3
        offset = offset + (lax.rem(key_cell, GW) - lax.rem(query_cell, GW) + 1)
        offset = jnp.clip(offset, 0, 26)
        for g in range(groups):
            value = table_ref[rank * groups + g, offset] * LOG2E
            bias_ref[t, i, g] = jnp.where(valid, value, -1e30)
        return 0

    lax.fori_loop(0, frame_tiles * slots, tabulate, 0)

    @pl.when(jnp.logical_not(leads))
    def _():
        for own in range(ahead):
            start_halo(*steps[own], range(1))

    for at in range(ahead - 1):
        for d in range(1, n):
            across(*steps[at], d).wait_recv()
        start_halo(*steps[at], range(1, n))


    pairs = slots // 2
    ones = jnp.ones((2 * TILE, DH), jnp.bfloat16)
    first = lax.div(lax.rem(rank + 1, n) * tokens, TILE)

    def listed(buf, t, p):
        return jnp.concatenate(
            [
                buf[lists_ref[t, 2 * p + i] * parts + j]
                for i in range(2)
                for j in range(parts)
            ],
            axis=0,
        )

    def weigh(g):
        def tile_body(t, _):
            here = pl.ds(pl.multiple_of(t * TILE, TILE), TILE)

            def score_pair(p, top):
                s = lax.dot_general(
                    q_bufs[g][here, :],
                    listed(k_bufs[g], t, p),
                    (((1,), (1,)), ((), ())),
                    preferred_element_type=jnp.float32,
                )
                s_buf[p] = s
                for i in range(2):
                    m = s[:, i * TILE : i * TILE + DH]
                    for c in range(1, TILE // DH):
                        m = jnp.maximum(m, s[:, i * TILE + c * DH : i * TILE + (c + 1) * DH])
                    top = jnp.maximum(top, m * scale + bias_ref[t, 2 * p + i, g])
                return top

            top = lax.fori_loop(0, pairs, score_pair, jnp.full((TILE, DH), -3e38, jnp.float32))
            top = jnp.broadcast_to(jnp.max(top, axis=1, keepdims=True), (TILE, DH))

            def weigh_pair(p, top):
                for i in range(2):
                    shift = bias_ref[t, 2 * p + i, g] - top
                    for c in range(TILE // DH):
                        span = slice(i * TILE + c * DH, i * TILE + (c + 1) * DH)
                        w = jnp.exp2(s_buf[p, :, span] * scale + shift)
                        w_buf[g % 2, t * pairs + p, :, span] = w.astype(jnp.bfloat16)
                return top

            lax.fori_loop(0, pairs, weigh_pair, top)
            return 0

        lax.fori_loop(0, frame_tiles, tile_body, 0)

    def mix(g):
        def tile_body(step, _):
            t = lax.rem(step + first, frame_tiles)
            total = None
            for p in range(pairs):
                value = jnp.concatenate([listed(v_bufs[g], t, p), ones], axis=1)
                part = jnp.dot(
                    w_buf[g % 2, t * pairs + p], value, preferred_element_type=jnp.float32
                )
                total = part if total is None else total + part
            result = (total[:, :DH] / total[:, DH:]).astype(jnp.bfloat16)
            for j in range(parts):
                u = t * parts + j
                piece = result[j * unit : (j + 1) * unit]
                owner = lax.div(u, held)

                @pl.when(owner == rank)
                def _():
                    out_ref[lax.rem(u, held), :, lanes(rank, g)] = piece

                @pl.when(owner != rank)
                def _():
                    o_bufs[g][u] = piece
                    give(g, u).start()
            return 0

        lax.fori_loop(0, frame_tiles, tile_body, 0)

    def drain_return(heads):
        for g in heads:
            for d in range(1, n):
                for at in range(held):
                    taken(g, lax.rem(rank + d, n), at).wait_recv()
            for u in range(n * held):
                @pl.when(rank != u // held)
                def _():
                    give(g, u).wait_send()

    def drain_halo(done):
        for way, present in ((0, has_up), (1, has_down)):
            @pl.when(present)
            def _():
                for which, g in done:
                    for d in range(n):
                        halo(which, g, d, way).wait_send()

    for at, (which, g) in enumerate(steps):
        if at + ahead - 1 < len(steps):
            relay(*steps[at + ahead - 1])
        if at + ahead < len(steps):
            start_halo(*steps[at + ahead], range(1))
        local(which, g).wait()
        if which == 0:
            local(2, g).wait()
            for d in range(1, n):
                across(2, g, d).wait_recv()
        if at == len(steps) - 1:
            for done in range(groups):
                for d in range(1, n):
                    for part in range(3):
                        across(part, done, d).wait_send()
            drain_return(range(max(groups - 2, 0)))
            drain_halo(steps[:-ahead])
        arrive(which, g)
        if which == 0:
            weigh(g)
        else:
            mix(g)

    drain_return(range(max(groups - 2, 0), groups))
    drain_halo(steps[-ahead:])


def write_kernel(x_ref, out_ref, sems):
    count = sems.shape[0]
    width = x_ref.shape[2] // count

    def copy(i):
        part = pl.ds(i * width, width)
        return pltpu.make_async_copy(x_ref.at[:, :, part], out_ref.at[:, :, part], sems.at[i])

    for i in range(count):
        copy(i).start()
    for i in range(count):
        copy(i).wait()


def on_device(queries, keys, values, rel_bias, tile_lists, tile_pos):
    n = lax.axis_size("ulysses")
    blk_count = lax.axis_size("blk")
    groups = H // n
    tokens = queries.shape[0]
    frame_tokens = tokens * n
    frame_tiles = frame_tokens // TILE
    slots = tile_lists.shape[1]

    hbm = pl.BlockSpec(memory_space=pl.ANY)
    vmem = lambda *shape: [pltpu.VMEM((*shape, DH), jnp.bfloat16)] * groups
    unit = math.gcd(tokens, TILE)
    held = tokens // unit
    split = (held, unit, queries.shape[1])
    dma = pltpu.SemaphoreType.DMA
    by_head = pl.pallas_call(
        functools.partial(attention_kernel, n, blk_count, groups, tokens, slots),
        out_shape=pltpu.VMEM(split, jnp.bfloat16),
        in_specs=[hbm] * 6,
        out_specs=pl.BlockSpec(memory_space=pltpu.VMEM),
        scratch_shapes=[
            *vmem(3 * frame_tokens // unit, unit),
            *vmem(3 * frame_tokens // unit, unit),
            *vmem(frame_tokens),
            *vmem(frame_tokens // unit, unit),
            pltpu.SMEM(tile_lists.shape[::-1], jnp.int32),
            pltpu.SMEM(tile_pos.shape, jnp.int32),
            pltpu.SMEM(rel_bias.shape, jnp.float32),
            dma((3,)),
            pltpu.SMEM((frame_tiles, slots), jnp.int32),
            pltpu.SMEM((frame_tiles, slots, groups), jnp.float32),
            pltpu.VMEM((slots // 2, TILE, 2 * TILE), jnp.float32),
            pltpu.VMEM((2, frame_tiles * slots // 2, TILE, 2 * TILE), jnp.bfloat16),
            dma((3, groups)),
            dma((3, groups, n)),
            dma((3, groups, n)),
            dma((2, 2, groups, n)),
            dma((2, 2, groups, n)),
            dma((groups, n * held)),
            dma((groups, n, held)),
        ],
        compiler_params=pltpu.CompilerParams(
            collective_id=0, has_side_effects=True, vmem_limit_bytes=54 * 1024 * 1024
        ),
        name="attend",
    )(tile_lists.T, tile_pos, rel_bias, queries, keys.reshape(split), values.reshape(split))
    out = pl.pallas_call(
        write_kernel,
        out_shape=jax.ShapeDtypeStruct(split, jnp.bfloat16),
        in_specs=[hbm],
        out_specs=hbm,
        scratch_shapes=[dma((4,))],
        compiler_params=pltpu.CompilerParams(vmem_limit_bytes=1024 * 1024),
        name="write",
    )(by_head)
    return out.reshape(queries.shape)


def solution(mesh):
    return jax.shard_map(
        on_device,
        mesh=mesh,
        in_specs=(
            P(("dp", "blk", "ulysses"), None),
            P(("dp", "blk", "ulysses"), None),
            P(("dp", "blk", "ulysses"), None),
            P(),
            P(),
            P(),
        ),
        out_specs=P(("dp", "blk", "ulysses"), None),
        check_vma=False,
    )
```
